32 devices in a mesh: grp: 4 (over y, x), blk: 8 (over z, core).
Axes of the slice: x: 2, y: 2, z: 4, core: 2. Of those that a mesh axis runs over, the one named last changes fastest.
Arguments:
- student: bfloat16 [6144, 1024], P(('grp', 'blk')), parts along dimension 0, may hold values from -6 to 6
- teacher: bfloat16 [6144, 1024], P(('grp', 'blk')), parts along dimension 0, may hold values from -6 to 6
Outputs:
- grad_student: float32 [6144, 1024], P(('grp', 'blk')), parts along dimension 0
The draws below stay inside these ranges and needn't reach their ends.
There are 4 independent parts, one for each index of `grp`. The reference program is written for one: setup_inputs(seed, part) draws one part's arguments, and reference() takes and returns one part's arrays. A program takes and returns all parts, laid end to end along the dimension named above; each array names one. Nothing has to cross between parts.
All inputs are finite; a program needn't handle non-finite values.
Results may differ from the reference program's by a relative error of at most 0.01.
Values may be sent and summed in bfloat16 or wider, within the bound.
No kernel may reach another device: no remote copies, remote signals or barrier semaphores. Data moves between devices by JAX's collectives and lax.ppermute only.
A program may use at most 128 MiB of HBM per device.

```python
import jax
import jax.numpy as jnp
from jax import lax

D = 1024
N = 1536


def shard_levels(stream_key, dims, pieces, low, largest):
    def one(dim, parts):
        draws = jax.random.uniform(jax.random.fold_in(jax.random.fold_in(stream_key, 6), dim), (parts,), jnp.float32, low / len(pieces), largest / len(pieces))
        return jnp.repeat(jnp.exp(draws), dims[dim] // parts).reshape((-1,) + (1,) * (len(dims) - dim - 1))

    loudness = one(*pieces[0])
    for cut in pieces[1:]:
        loudness = loudness * one(*cut)
    return loudness


def centred(own_key, dims, width, bound, cuts=(), dtype=jnp.bfloat16):
    entries = width * jax.random.normal(own_key, dims, jnp.float32)
    if cuts:
        entries = entries * shard_levels(own_key, dims, cuts, -0.22, 0.18)
    return jnp.clip(entries, -bound, bound).astype(dtype)


def setup_inputs(seed: int = 0, part: int = 0) -> dict:
    key_list = jax.random.split(jax.random.key(seed), 3)
    own_keys = jax.random.split(jax.random.fold_in(key_list[2], part), 3)
    return {
        "student": centred(own_keys[0], (N, D), 1.0, 6.0, ((0, 8),)),
        "teacher": centred(own_keys[1], (N, D), 1.0, 6.0, ((0, 8),)),
    }


def normalize(values):
    floats = values.astype(jnp.float32)
    norms = jnp.sqrt(lax.optimization_barrier(jnp.sum(floats * floats, axis=1, keepdims=True)) + 1e-06)
    return (floats / norms, norms)

def split_product(left, right):
    left_hi = left.astype(jnp.bfloat16)
    left_lo = (left - left_hi.astype(jnp.float32)).astype(jnp.bfloat16)
    return jnp.dot(left_hi, right, preferred_element_type=jnp.float32) + jnp.dot(left_lo, right, preferred_element_type=jnp.float32)

def reference(student, teacher):
    s_float, norm_h = normalize(student)
    s_half = s_float.astype(jnp.bfloat16)
    t_float, teacher_norm = normalize(teacher)
    t_half = t_float.astype(jnp.bfloat16)
    gram_s = jnp.dot(s_half, s_half.T, preferred_element_type=jnp.float32)
    gram_t = jnp.dot(t_half, t_half.T, preferred_element_type=jnp.float32)
    diff = gram_s - gram_t
    s_wide = s_half.astype(jnp.float32)
    product = split_product(diff, s_half)
    g_s = product * (D / jnp.sqrt(jnp.float32(N)))
    along = lax.optimization_barrier(jnp.sum(s_wide * g_s, axis=1, keepdims=True))
    return (g_s - s_wide * along) / norm_h
```

```python
import functools

import jax
import jax.numpy as jnp
from jax import lax
from jax.experimental import pallas as pl
from jax.experimental.pallas import tpu as pltpu
from jax.sharding import PartitionSpec as P

CORES = 2
VMEM = pltpu.MemorySpace.VMEM
SMEM = pltpu.MemorySpace.SMEM
NT = (((1,), (1,)), ((), ()))


def normalized(ref):
    floats = ref[...].astype(jnp.float32)
    norms = jnp.sqrt(jnp.sum(floats * floats, axis=1, keepdims=True) + 1e-06)
    return (floats / norms).astype(jnp.bfloat16), norms


def accumulate(s_rows, t_rows, s_cols, t_cols, store):
    slab = s_cols.shape[0]
    for start in range(0, s_rows.shape[0], slab):
        rows = pl.ds(start, slab)
        gram = lax.dot_general(
            s_rows[rows, :], s_cols[...], NT, preferred_element_type=jnp.float32
        ) - lax.dot_general(
            t_rows[rows, :], t_cols[...], NT, preferred_element_type=jnp.float32
        )
        high = gram.astype(jnp.bfloat16)
        low = (gram - high.astype(jnp.float32)).astype(jnp.bfloat16)
        store(
            rows,
            jnp.dot(high, s_cols[...], preferred_element_type=jnp.float32)
            + jnp.dot(low, s_cols[...], preferred_element_type=jnp.float32),
        )


def first_kernel(s_own, t_own, s_other, t_other, s_rows, t_rows, norms, total):
    half = s_own.shape[0]
    own, other = pl.ds(0, half), pl.ds(half, half)
    s_rows[own, :], norm = normalized(s_own)
    norms[...] = jnp.broadcast_to(norm, norms.shape)
    t_rows[own, :], _ = normalized(t_own)
    s_rows[other, :], _ = normalized(s_other)
    t_rows[other, :], _ = normalized(t_other)

    def store(rows, value):
        total[rows, :] = value

    accumulate(s_rows, t_rows, s_rows.at[own, :], t_rows.at[own, :], store)


def step_kernel(
    low_ok, high_ok, place, s_rows, t_rows, total_in, s_right, t_right, s_left, t_left,
    total, s_raw, t_raw, s_cols, t_cols, sems,
):
    @pl.when(pl.program_id(0) == 0)
    def _():
        total[...] = total_in[...]

    def block(s_hbm, t_hbm):
        s_copy = pltpu.make_async_copy(s_hbm, s_raw, sems.at[0])
        t_copy = pltpu.make_async_copy(t_hbm, t_raw, sems.at[1])
        s_copy.start()
        t_copy.start()
        s_copy.wait()
        s_cols[...], _ = normalized(s_raw)
        t_copy.wait()
        t_cols[...], _ = normalized(t_raw)

        def store(rows, value):
            total[rows, :] += value

        accumulate(s_rows, t_rows, s_cols, t_cols, store)

    chip = place[0]

    @pl.when(chip >= low_ok)
    def _():
        block(s_right, t_right)

    @pl.when(chip <= high_ok)
    def _():
        block(s_left, t_left)


def last_kernel(scale, total, received, s_rows, norms, out):
    g_s = (total[...] + received[...]) * scale
    s_wide = s_rows[...].astype(jnp.float32)
    along = jnp.sum(s_wide * g_s, axis=1, keepdims=True)
    out[...] = (g_s - s_wide * along) / norms[:, :1]


def cost(rows, cols, width, bytes_accessed):
    return pl.CostEstimate(
        flops=8 * rows * cols * width, bytes_accessed=bytes_accessed, transcendentals=0
    )


def body(student, teacher):
    half, width = student.shape
    devices = lax.axis_size("blk")
    chips = devices // CORES
    rows = CORES * half
    text_count = half * devices
    bf16, f32 = jnp.bfloat16, jnp.float32
    vmem = pl.BlockSpec(memory_space=VMEM)
    anywhere = pl.BlockSpec(memory_space=pl.ANY)
    place = (lax.axis_index("blk") // CORES).reshape(1)

    def hop(value, shift, sources):
        pairs = [
            (CORES * i + c, CORES * (i + shift) + c) for i in sources for c in range(CORES)
        ]
        return lax.ppermute(value, "blk", pairs)

    def partner(value):
        return lax.ppermute(value, "blk", [(i, i ^ 1) for i in range(devices)])

    right, left, steps = (student, teacher), (student, teacher), []
    for step in range(1, chips):
        r_src, l_src = range(step - 1, chips - 1), range(1, chips - step + 1)
        s_pair = hop(right[0], 1, r_src), hop(left[0], -1, l_src)
        t_pair = hop(right[1], 1, r_src), hop(left[1], -1, l_src)
        right, left = (s_pair[0], t_pair[0]), (s_pair[1], t_pair[1])
        steps.append(right + left)

    s_other, t_other = partner(student), partner(teacher)
    s_rows, t_rows, norms, total = pl.pallas_call(
        first_kernel,
        out_shape=(
            jax.ShapeDtypeStruct((rows, width), bf16),
            jax.ShapeDtypeStruct((rows, width), bf16),
            jax.ShapeDtypeStruct((half, 128), f32),
            jax.ShapeDtypeStruct((rows, width), f32),
        ),
        in_specs=[vmem] * 4,
        out_specs=(vmem,) * 4,
        cost_estimate=cost(rows, half, width, 12 * rows * width),
    )(student, teacher, s_other, t_other)
    for step, blocks in enumerate(steps, 1):
        total = pl.pallas_call(
            functools.partial(step_kernel, step, chips - 1 - step),
            grid=(1,),
            out_shape=jax.ShapeDtypeStruct((rows, width), f32),
            in_specs=[pl.BlockSpec(memory_space=SMEM)] + [vmem] * 3 + [anywhere] * 4,
            out_specs=vmem,
            scratch_shapes=[pltpu.VMEM((half, width), bf16)] * 4
            + [pltpu.SemaphoreType.DMA((2,))],
            cost_estimate=cost(rows, 2 * half, width, 12 * rows * width),
        )(place, s_rows, t_rows, total, *blocks)
    received = partner(total[half:])
    return pl.pallas_call(
        functools.partial(last_kernel, width / text_count**0.5),
        grid=(1,),
        out_shape=jax.ShapeDtypeStruct((half, width), f32),
        in_specs=[
            pl.BlockSpec((half, width), lambda i: (0, 0)),
            pl.BlockSpec((half, width), lambda i: (0, 0)),
            pl.BlockSpec((half, width), lambda i: (0, 0)),
            pl.BlockSpec((half, 128), lambda i: (0, 0)),
        ],
        out_specs=pl.BlockSpec((half, width), lambda i: (0, 0)),
    )(total, received, s_rows, norms)


def solution(mesh):
    in_specs = (P(("grp", "blk"), None), P(("grp", "blk"), None))
    out_specs = P(("grp", "blk"), None)
    return jax.shard_map(body, mesh=mesh, in_specs=in_specs, out_specs=out_specs, check_vma=False)
```

```python
import functools

import jax
import jax.numpy as jnp
from jax import lax
from jax.experimental import pallas as pl
from jax.experimental.pallas import tpu as pltpu
from jax.sharding import PartitionSpec as P


CORES = 2
VMEM = pltpu.MemorySpace.VMEM
SMEM = pltpu.MemorySpace.SMEM
NT = (((1,), (1,)), ((), ()))
TN = (((0,), (0,)), ((), ()))
GRANT = 16 * 2**20


def dot(left, right, dims=(((1,), (0,)), ((), ()))):
    return lax.dot_general(left, right, dims, preferred_element_type=jnp.float32)


def normalized(ref):
    floats = ref[...].astype(jnp.float32)
    norms = jnp.sqrt(jnp.sum(floats * floats, axis=1, keepdims=True) + 1e-06)
    return (floats / norms).astype(jnp.bfloat16), norms


def gram(s_rows, t_rows, s_cols, t_cols):
    return dot(s_rows, s_cols, NT) - dot(t_rows, t_cols, NT)


def accumulate(s_rows, t_rows, s_cols, t_cols, totals, fresh=False):
    half = s_cols.shape[0]
    for index, total in enumerate(totals):
        rows = pl.ds(index * half, half)
        block = gram(s_rows[rows, :], t_rows[rows, :], s_cols[...], t_cols[...])
        high = block.astype(jnp.bfloat16)
        low = (block - high.astype(jnp.float32)).astype(jnp.bfloat16)
        product = dot(high, s_cols[...]) + dot(low, s_cols[...])
        total[...] = product if fresh else total[...] + product


def normalize_pair(first, second, out):
    half = first.shape[0]
    out[pl.ds(0, half), :], norm = normalized(first)
    out[pl.ds(half, half), :], _ = normalized(second)
    return norm


def first_kernel(s_own, t_own, s_other, t_other, s_rows, t_rows, norms, mine, theirs):
    own = pl.ds(0, s_own.shape[0])
    norm = normalize_pair(s_own, s_other, s_rows)
    norms[...] = jnp.broadcast_to(norm, norms.shape)
    normalize_pair(t_own, t_other, t_rows)
    accumulate(
        s_rows, t_rows, s_rows.at[own, :], t_rows.at[own, :], (mine, theirs), fresh=True
    )


def end_rows_kernel(s_own, t_own, s_other, t_other, s_end, t_end):
    normalize_pair(s_own, s_other, s_end)
    normalize_pair(t_own, t_other, t_end)


def end_block_kernel(next_to_end, s_end, t_end, s_block, t_block, e_out):
    @pl.when(next_to_end[0] > 0)
    def _():
        s_cols, _ = normalized(s_block)
        t_cols, _ = normalized(t_block)
        e_out[...] = gram(s_cols, t_cols, s_end[...], t_end[...]).astype(e_out.dtype)


def last_block_kernel(next_to_end, s_end, t_end, s_block, t_block, same, cross):
    @pl.when(next_to_end[0] > 0)
    def _():
        half = s_block.shape[0]
        s_cols, _ = normalized(s_block)
        t_cols, _ = normalized(t_block)
        for index, out in enumerate((same, cross)):
            rows = pl.ds(index * half, half)
            block = gram(s_end[rows, :], t_end[rows, :], s_cols, t_cols)
            out[...] = block.astype(out.dtype)


def step_kernel(kinds, oks, s_rows, t_rows, mine_in, theirs_in, *refs):
    half = mine_in.shape[0]
    blocks, (mine, theirs, s_cols, t_cols) = refs[:-4], refs[-4:]
    for index, ready in enumerate(kinds):
        s_block, other = blocks[2 * index], blocks[2 * index + 1]

        @pl.when(oks[index] > 0)
        def _(s_block=s_block, other=other, ready=ready):
            s_cols[...], _ = normalized(s_block)
            if ready:
                for place, total in enumerate((mine, theirs)):
                    part = other[:, place * half : (place + 1) * half]
                    total[...] += dot(part, s_cols[...], TN)
            else:
                t_cols[...], _ = normalized(other)
                accumulate(s_rows, t_rows, s_cols, t_cols, (mine, theirs))


def sum_kernel(at_end, mine, received, s_near, s_far, total, s_last):
    total[...] = mine[...] + received[...]

    @pl.when(at_end[0] > 0)
    def _():
        normalize_pair(s_near, s_far, s_last)


def last_kernel(scale, at_end, total, s_rows, norms, s_last, same, cross, out, g_s):
    half = total.shape[0]
    g_s[...] = total[...]

    @pl.when(at_end[0] > 0)
    def _():
        g_s[...] += dot(same[...], s_last[pl.ds(0, half), :]) + dot(
            cross[...], s_last[pl.ds(half, half), :]
        )

    scaled = g_s[...] * scale
    s_wide = s_rows[pl.ds(0, half), :].astype(jnp.float32)
    along = jnp.sum(s_wide * scaled, axis=1, keepdims=True)
    out[...] = (scaled - s_wide * along) / norms[:, :1]


def cost(rows, cols, width):
    return pl.CostEstimate(
        flops=8 * rows * cols * width, bytes_accessed=8 * rows * width, transcendentals=0
    )


def body(student, teacher):
    half, width = student.shape
    devices = lax.axis_size("blk")
    chips = devices // CORES
    rows = CORES * half
    text_count = half * devices
    bf16, f32 = jnp.bfloat16, jnp.float32
    shape = jax.ShapeDtypeStruct
    vmem = pl.BlockSpec(memory_space=VMEM)
    smem = pl.BlockSpec(memory_space=SMEM)
    chip = lax.div(lax.axis_index("blk"), CORES)
    flag = lambda value: value.astype(jnp.int32).reshape(1)
    at_end = (chip == 0) | (chip == chips - 1)
    next_to_end = flag((chip == 1) | (chip == chips - 2))
    at_end = flag(at_end)
    ends = (0, chips - 1)

    def call(kernel, outs, *args, flags=0, cols=half, **options):
        return run(kernel, outs, *args, flags=flags, cols=cols, **options)

    def run(kernel, outs, *args, flags, cols, **options):
        return pl.pallas_call(
            kernel,
            out_shape=outs,
            in_specs=[smem] * flags + [vmem] * (len(args) - flags),
            out_specs=jax.tree.map(lambda _: vmem, outs),
            compiler_params=pltpu.CompilerParams(vmem_limit_bytes=GRANT),
            cost_estimate=cost(rows, cols, width),
            **options,
        )(*args)

    def permute(value, pairs, cross=0):
        cores = [(CORES * a + c, CORES * b + (c ^ cross)) for a, b in pairs for c in range(CORES)]
        return lax.ppermute(value, "blk", cores)

    def partner(value, among=range(chips)):
        return permute(value, [(i, i) for i in among], cross=1)

    def links(step, parity):
        for low in range(parity, chips - 1, 2):
            if low - step + 1 >= 0:
                yield low, low + 1
            if low + step <= chips - 1:
                yield low + 1, low

    inner = [i for i in (1, chips - 2)]
    s_rows, t_rows, norms, mine, theirs = call(
        first_kernel,
        (
            shape((rows, width), bf16),
            shape((rows, width), bf16),
            shape((half, 128), f32),
            shape((half, width), f32),
            shape((half, width), f32),
        ),
        student,
        teacher,
        partner(student),
        partner(teacher),
    )

    held = ((student, teacher),) * 2
    e_block = None
    for step in range(1, chips - 1):
        moved, kinds, oks, blocks = [], [], [], []
        for parity in range(2):
            moves = list(links(step, parity))
            before = held[1 - parity]
            through = [m for m in moves if step == 1 or m[1] not in ends]
            s_block = permute(before[0], moves) if moves else None
            t_block = permute(before[1], through) if through else None
            moved.append((s_block, t_block))
            up = lax.rem(chip, 2) == parity
            here = jnp.where(up, chip + step <= chips - 1, chip >= step)
            if through:
                kinds.append(False)
                oks.append(here & (at_end[0] == 0) if step > 1 else here)
                blocks.extend((s_block, t_block))
            if len(through) < len(moves):
                kinds.append(True)
                oks.append(here & (at_end[0] > 0))
                e_here = permute(e_block, [m for m in moves if m[1] in ends])
                blocks.extend((s_block, e_here))
        held = tuple(moved)
        if step == 1:
            first = held[0]
            s_end, t_end = call(
                end_rows_kernel,
                (shape((rows, width), bf16),) * 2,
                *first,
                partner(first[0], inner),
                partner(first[1], inner),
            )
        if step < chips - 2:
            e_block = call(
                end_block_kernel,
                shape((half, rows), bf16),
                next_to_end, s_end, t_end, *held[1],
                flags=1,
            )
        else:
            same, cross = call(
                last_block_kernel,
                (shape((half, half), bf16),) * 2,
                next_to_end, s_end, t_end, *held[1],
                flags=1,
            )
        mine, theirs = call(
            functools.partial(step_kernel, tuple(kinds)),
            (shape((half, width), f32),) * 2,
            jnp.stack(oks).astype(jnp.int32), s_rows, t_rows, mine, theirs, *blocks,
            flags=1,
            input_output_aliases={3: 0, 4: 1},
            scratch_shapes=[pltpu.VMEM((half, width), bf16)] * 2,
        )
    last = [(1, 0), (chips - 2, chips - 1)]
    s_last = permute(held[1][0], last)
    same = permute(same, last)
    cross = permute(cross, last, cross=1)
    total, s_last = call(
        sum_kernel,
        (shape((half, width), f32), shape((rows, width), bf16)),
        at_end, mine, partner(theirs), s_last, partner(s_last, ends),
        flags=1,
    )
    return call(
        functools.partial(last_kernel, width / text_count**0.5),
        shape((half, width), f32),
        at_end, total, s_rows, norms, s_last, same, cross,
        flags=1,
        scratch_shapes=[pltpu.VMEM((half, width), f32)],
    )


def solution(mesh):
    rows = P(("grp", "blk"), None)
    return jax.shard_map(
        body, mesh=mesh, in_specs=(rows, rows), out_specs=rows, check_vma=False
    )
```
